768 devices in a mesh: dp: 48 (over z, x), fsdp: 16 (over y, core).
Axes of the slice: x: 4, y: 8, z: 12, core: 2. Of those that a mesh axis runs over, the one named last changes fastest.
Arguments:
- frames: bfloat16 [48, 16, 576, 1024], P('dp', 'fsdp'), may hold values from -6 to 6
- route: int32 [48, 16, 576], P('dp', 'fsdp'), may hold values from 0 to 575, each once within a row
- valid: int32 [48, 16, 576], P('dp', 'fsdp'), may hold values 0 or 1
- w_pw: bfloat16 [1024, 2048], P('fsdp'), may hold values from -0.1875 to 0.1875
- cotangent: bfloat16 [48, 16, 576, 1024], P('dp', 'fsdp'), may hold values from -6 to 6
Outputs:
- gated: bfloat16 [48, 16, 576, 1024], P('dp', 'fsdp')
- grad_pw: bfloat16 [48, 1024, 2048], P('dp', 'fsdp')
The draws below stay inside these ranges and needn't reach their ends.
Inputs may be any that keep to these rules, and one draw needn't show every extreme that they name: Each row of route is a permutation of the frames of one device.
All inputs are finite; a program needn't handle non-finite values. No bound on the sum of `valid` on one device may be relied on, other than what follows from the above.
Results may differ from the reference program's by a relative error of at most 0.017.
Values may be sent and summed in bfloat16 or wider, within the bound.
No kernel may reach another device: no remote copies, remote signals or barrier semaphores. Data moves between devices by JAX's collectives and lax.ppermute only.
A program may use at most 32 MiB of HBM per device.

```python
import jax
import jax.numpy as jnp
from jax import lax

D = 1024
ROWS_DEV = 576
N_DP = 48
N_FSDP = 16


def touch_ends(drawn, key, smallest, largest):
    spot = [jax.random.randint(jax.random.fold_in(key, axis), (), 0, length) for axis, length in enumerate(drawn.shape)]
    main_axis = drawn.shape.index(max(drawn.shape))
    neighbour = spot[:main_axis] + [(spot[main_axis] + 1) % drawn.shape[main_axis]] + spot[main_axis + 1:]
    return drawn.at[tuple(spot)].set(smallest).at[tuple(neighbour)].set(largest)


def block_scale(stream_key, shape, cuts, least, high):
    def one(position, shards_of):
        steps = jax.random.uniform(jax.random.fold_in(jax.random.fold_in(stream_key, 6), position), (shards_of,), jnp.float32, least / len(cuts), high / len(cuts))
        return jnp.repeat(jnp.exp(steps), shape[position] // shards_of).reshape((-1,) + (1,) * (len(shape) - position - 1))

    factor_of = one(*cuts[0])
    for cut in cuts[1:]:
        factor_of = factor_of * one(*cut)
    return factor_of


def scatter_about(key, shape, scale, reach, split=(), kind=jnp.bfloat16):
    array = scale * jax.random.normal(key, shape, jnp.float32)
    if split:
        array = array * block_scale(key, shape, split, -0.22, 0.18)
    return jnp.clip(array, -reach, reach).astype(kind)


def setup_inputs(seed: int = 0) -> dict:
    arg_keys = jax.random.split(jax.random.key(seed), 6)
    return {
        "frames": scatter_about(arg_keys[0], (N_DP, N_FSDP, ROWS_DEV, D), 1.0, 6.0, ((0, 48), (1, 16))),
        "route": jax.vmap(lambda own: jax.random.permutation(own, ROWS_DEV))(jax.random.split(arg_keys[1], N_DP * N_FSDP)).reshape((N_DP, N_FSDP, ROWS_DEV)).astype(jnp.int32),
        "valid": touch_ends((jax.random.randint(arg_keys[2], (N_DP, N_FSDP, ROWS_DEV), 0, 4) < 3).astype(jnp.int32), jax.random.fold_in(arg_keys[2], 1), 0, 1),
        "w_pw": scatter_about(arg_keys[3], (D, 2 * D), D ** -0.5, 0.1875, ((0, 16),)),
        "cotangent": scatter_about(arg_keys[4], (N_DP, N_FSDP, ROWS_DEV, D), 1.0, 6.0, ((0, 48), (1, 16))),
    }


def reference(frames, route, valid, w_pw, cotangent):
    picked = jnp.take_along_axis(frames, route[..., None], axis=2)
    keep = jnp.take_along_axis(valid, route, axis=2)
    sent = jnp.where(keep[..., None] > 0, picked, jnp.zeros_like(picked)).astype(jnp.bfloat16)
    width = frames.shape[3]
    blocks = sent.reshape(N_DP, N_FSDP, N_DP, ROWS_DEV // N_DP, width)
    received = jnp.transpose(blocks, (2, 1, 0, 3, 4)).reshape(N_DP, N_FSDP, ROWS_DEV, width)

    def group(pair):
        rows, grads = pair
        values = rows.astype(jnp.float32)
        mean = lax.optimization_barrier(jnp.mean(values, axis=-1, keepdims=True))
        centred = values - mean
        variance = lax.optimization_barrier(jnp.mean(centred * centred, axis=-1, keepdims=True))
        normed = (centred * lax.rsqrt(variance + 1e-05)).astype(jnp.bfloat16)
        flat = normed.reshape(N_FSDP * ROWS_DEV, width)
        pre = jnp.dot(flat, w_pw, preferred_element_type=jnp.float32)
        first = pre[:, :width]
        second = jax.nn.sigmoid(pre[:, width:])
        gated = (first * second).astype(jnp.bfloat16)
        upstream = grads.reshape(N_FSDP * ROWS_DEV, width).astype(jnp.float32)
        dpre = jnp.concatenate([upstream * second, upstream * first * second * (1.0 - second)], axis=1).astype(jnp.bfloat16)
        total = jnp.zeros((width, 2 * width), jnp.float32)
        for index in range(N_FSDP):
            lower = index * ROWS_DEV
            part = lax.dot_general(flat[lower:lower + ROWS_DEV], dpre[lower:lower + ROWS_DEV], (((0,), (0,)), ((), ())), preferred_element_type=jnp.float32)
            total = total + part.astype(jnp.bfloat16).astype(jnp.float32)
        return (gated.reshape(N_FSDP, ROWS_DEV, width), total.astype(jnp.bfloat16))
    gated, grad_pw = lax.map(group, (received, cotangent))
    return (gated, grad_pw)
```

```python
import jax
import jax.numpy as jnp
from jax import lax
from jax.experimental import pallas as pl
from jax.experimental.pallas import tpu as pltpu
from jax.sharding import Mesh, PartitionSpec as P


BF, F32 = jnp.bfloat16, jnp.float32


def spread(half, transposed=False):
    shape = (192, 96) if transposed else (96, 192)
    narrow = lax.broadcasted_iota(jnp.int32, shape, 1 if transposed else 0)
    wide = lax.broadcasted_iota(jnp.int32, shape, 0 if transposed else 1)
    hit = wide == narrow + (narrow // 12 + half) * 12
    return jnp.where(hit, 1.0, 0.0).astype(BF)


def pick_kernel(route_ref, valid_ref, frames_ref, out_ref):
    rows = frames_ref.shape[0]
    lane = lax.broadcasted_iota(jnp.int32, (rows, rows), 1)
    sub = lax.broadcasted_iota(jnp.int32, (rows, rows), 0)
    order = jnp.sum(jnp.where(lane == sub, route_ref[...].astype(F32), 0.0), axis=1, keepdims=True)
    hit = (lane == order.astype(jnp.int32)) & (valid_ref[...] > 0)
    chosen = jnp.where(hit, 1.0, 0.0).astype(BF)
    values = jnp.dot(chosen, frames_ref[...], preferred_element_type=F32)
    mean = jnp.mean(values, axis=-1, keepdims=True)
    centred = values - mean
    variance = jnp.mean(centred * centred, axis=-1, keepdims=True)
    normed = (centred * lax.rsqrt(variance + 1e-05)).astype(BF)
    low, high = spread(0, True), spread(1, True)
    for b in range(rows // 96):
        part = normed[b * 96:(b + 1) * 96]
        both = jnp.dot(low, part[:, :512], preferred_element_type=F32)
        both += jnp.dot(high, part[:, 512:], preferred_element_type=F32)
        out_ref[b * 192:(b + 1) * 192, :] = both.astype(BF)


def gate(normed, flip, wa_ref, wb_ref, cot_ref, gated_ref, keep_ref, send_ref):
    first = jnp.dot(normed, wa_ref[...], preferred_element_type=F32)
    second = jax.nn.sigmoid(jnp.dot(normed, wb_ref[...], preferred_element_type=F32))
    gated = first * second
    gated_ref[...] = gated.astype(BF)
    upstream = cot_ref[...].astype(F32)
    da = (upstream * second).astype(BF)
    db = (upstream * gated * (1.0 - second)).astype(BF)
    for h, slope in enumerate((da, db)):
        grad = jnp.dot(flip, slope, preferred_element_type=F32).astype(BF)
        keep_ref[0, h], keep_ref[1, h] = grad[:256], grad[256:512]
        send_ref[0, h], send_ref[1, h] = grad[512:768], grad[768:]


def first_kernel(pos_ref, got_ref, wa_ref, wb_ref, cot_ref, gated_ref, keep_ref, send_ref, normed_ref, flip_ref):
    @pl.when(pl.program_id(0) == 0)
    def _():
        low, high = spread(0), spread(1)
        for b in range(6):
            part = got_ref[b * 192:(b + 1) * 192, :]
            normed_ref[b * 96:(b + 1) * 96, :512] = jnp.dot(low, part, preferred_element_type=F32).astype(BF)
            normed_ref[b * 96:(b + 1) * 96, 512:] = jnp.dot(high, part, preferred_element_type=F32).astype(BF)
        for f in range(0, 16, 2):
            turned = normed_ref[:, f * 64:f * 64 + 128].T
            flip_ref[pos_ref[f]] = turned[:64]
            flip_ref[pos_ref[f + 1]] = turned[64:]

    flip = flip_ref[...].reshape(1024, 576)
    gate(normed_ref[...], flip, wa_ref, wb_ref, cot_ref, gated_ref, keep_ref, send_ref)


def second_kernel(pos_ref, normed_ref, flip_ref, wa_ref, wb_ref, cot_ref, _, gated_ref, keep_ref, send_ref):
    flip = flip_ref[...].reshape(1024, 576)
    gate(normed_ref[...], flip, wa_ref, wb_ref, cot_ref, gated_ref, keep_ref, send_ref)


COLS = 256
STEPS = 512 // COLS


def half_call(pos, lead, w, cot, gated=None):
    second = gated is not None
    fixed = lambda shape: pl.BlockSpec(shape, lambda j, p: (0,) * len(shape))
    wide = pl.BlockSpec((576, COLS), lambda j, p: (0, p[16] * STEPS + j))
    grad = pl.BlockSpec((2, 2, 256, COLS), lambda j, p: (0, 0, 0, j))
    in_specs = [fixed(a.shape) for a in lead]
    in_specs += [pl.BlockSpec((1024, COLS), lambda j, p: (0, j)), pl.BlockSpec((1024, COLS), lambda j, p: (0, j + STEPS)), wide]
    out_specs = [wide] + [grad] * 2
    out_shape = [jax.ShapeDtypeStruct((576, 1024), BF)] + [jax.ShapeDtypeStruct((2, 2, 256, 512), BF)] * 2
    args = [pos, *lead, w, w, cot]
    alias = {}
    if second:
        in_specs.append(pl.BlockSpec(memory_space=pl.ANY))
        alias = {len(args): 0}
        args.append(gated)
    else:
        out_specs += [fixed((576, 1024)), fixed((16, 64, 576))]
        out_shape += [jax.ShapeDtypeStruct((576, 1024), BF), jax.ShapeDtypeStruct((16, 64, 576), BF)]
    gs = pltpu.PrefetchScalarGridSpec(num_scalar_prefetch=1, grid=(STEPS,), in_specs=in_specs, out_specs=out_specs)
    return pl.pallas_call(
        second_kernel if second else first_kernel,
        grid_spec=gs,
        out_shape=out_shape,
        input_output_aliases=alias,
        compiler_params=pltpu.CompilerParams(vmem_limit_bytes=40 << 20),
        name="second" if second else "first",
    )(*args)


def add(u, v):
    return (u.astype(F32) + v.astype(F32)).astype(BF)


def add3(u, v, t):
    return (u.astype(F32) + v.astype(F32) + t.astype(F32)).astype(BF)


def body(frames, route, valid, w_pw, cotangent):
    y, c = lax.axis_index("y"), lax.axis_index("c")
    swap = [(0, 1), (1, 0)]
    shift = lambda d: [(i, (i + d) % 8) for i in range(8)]
    right = [(i, i ^ 1) for i in range(8)]
    left = [(i, (i + 1) % 8 if i % 2 else (i - 1) % 8) for i in range(8)]

    mate = lax.ppermute(w_pw, "c", swap)
    rows = jnp.where(c == 0, jnp.concatenate([w_pw, mate]), jnp.concatenate([mate, w_pw]))
    quarter = [rows[:, q * 512:(q + 1) * 512] for q in range(4)]
    mine = jnp.concatenate([jnp.where(c == 0, quarter[0], quarter[1]), jnp.where(c == 0, quarter[2], quarter[3])], axis=1)

    out = pl.pallas_call(
        pick_kernel,
        out_shape=jax.ShapeDtypeStruct((1152, 512), BF),
        compiler_params=pltpu.CompilerParams(vmem_limit_bytes=30 << 20),
        name="pick",
    )(route[0], valid[0], frames[0, 0])
    got = lax.all_to_all(out.reshape(48, 24, 512), ("z", "x"), 0, 0, tiled=True).reshape(1152, 512)

    same = jnp.zeros((4, 128, 1024), BF)
    for d in (0, 2, 6, 4):
        piece = lax.ppermute(mine, "y", shift(d)) if d else mine
        same = lax.dynamic_update_slice(same, piece[None], (((y - d) & 7) >> 1, 0, 0))
    cross = jnp.concatenate([lax.ppermute(same[:2], "y", right), lax.ppermute(same[2:], "y", left)])
    pair = jnp.where((y & 1) == 0, jnp.stack([same, cross], axis=1), jnp.stack([cross, same], axis=1))
    w_own = pair.reshape(1024, 1024)
    w_mate = lax.ppermute(w_own, "c", swap)

    f = jnp.arange(16, dtype=jnp.int32)
    pos = ((f & 1) ^ c) * 8 + (((f >> 1) & 1) ^ (y & 1)) * 4 + (f >> 2)
    pos_own = jnp.concatenate([pos, c[None]]).astype(jnp.int32)
    pos_mate = jnp.concatenate([pos, 1 - c[None]]).astype(jnp.int32)
    cot = cotangent[0, 0]
    gated, own, send_own, normed, flip = half_call(pos_own, (got,), w_own, cot)
    got_other = lax.ppermute(send_own, "c", swap)
    gated, other, send_other = half_call(pos_mate, (normed, flip), w_mate, cot, gated)
    got_own = lax.ppermute(send_other, "c", swap)
    peer = lax.ppermute(add(other[1], got_other[1]), "y", right)
    other = add3(other[0], got_other[0], peer)
    peer = lax.ppermute(add(own[1], got_own[1]), "y", left)
    own = add3(own[0], got_own[0], peer)
    both = jnp.concatenate([g.reshape(2, 4, 64, 512)[h] for g in (own, other) for h in (0, 1)], axis=2)
    parts = lax.all_to_all(both, "y", 0, 0, tiled=True, axis_index_groups=[[0, 2, 4, 6], [1, 3, 5, 7]])
    grad = jnp.sum(parts.astype(F32), axis=0).astype(BF)
    oa, ob, ma, mb = (grad[:, q * 512:(q + 1) * 512] for q in range(4))
    grad = jnp.where(c == 0, jnp.concatenate([oa, ma, ob, mb], axis=1), jnp.concatenate([ma, oa, mb, ob], axis=1))
    return gated[None, None], grad[None]


def solution(mesh):
    fine = Mesh(mesh.devices.reshape(12, 4, 8, 2), ("z", "x", "y", "c"))
    dp, fsdp = ("z", "x"), ("y", "c")
    in_specs = (P(dp, fsdp), P(dp, fsdp), P(dp, fsdp), P(fsdp), P(dp, fsdp))
    return jax.shard_map(body, mesh=fine, in_specs=in_specs, out_specs=(P(dp, fsdp), P(dp, fsdp)), check_vma=False)
```

```python
import jax
import jax.numpy as jnp
from jax import lax
from jax.experimental import pallas as pl
from jax.experimental.pallas import tpu as pltpu
from jax.sharding import Mesh, PartitionSpec as P


BF, F32 = jnp.bfloat16, jnp.float32


def spread(half, transposed=False):
    shape = (192, 96) if transposed else (96, 192)
    narrow = lax.broadcasted_iota(jnp.int32, shape, 1 if transposed else 0)
    wide = lax.broadcasted_iota(jnp.int32, shape, 0 if transposed else 1)
    hit = wide == narrow + (narrow // 12 + half) * 12
    return jnp.where(hit, 1.0, 0.0).astype(BF)


def pick_kernel(route_ref, valid_ref, frames_ref, out_ref):
    rows = frames_ref.shape[0]
    lane = lax.broadcasted_iota(jnp.int32, (rows, rows), 1)
    sub = lax.broadcasted_iota(jnp.int32, (rows, rows), 0)
    order = jnp.sum(jnp.where(lane == sub, route_ref[...].astype(F32), 0.0), axis=1, keepdims=True)
    hit = (lane == order.astype(jnp.int32)) & (valid_ref[...] > 0)
    chosen = jnp.where(hit, 1.0, 0.0).astype(BF)
    values = jnp.dot(chosen, frames_ref[...], preferred_element_type=F32)
    mean = jnp.mean(values, axis=-1, keepdims=True)
    centred = values - mean
    variance = jnp.mean(centred * centred, axis=-1, keepdims=True)
    normed = (centred * lax.rsqrt(variance + 1e-05)).astype(BF)
    low, high = spread(0, True), spread(1, True)
    for b in range(rows // 96):
        part = normed[b * 96:(b + 1) * 96]
        both = jnp.dot(low, part[:, :512], preferred_element_type=F32)
        both += jnp.dot(high, part[:, 512:], preferred_element_type=F32)
        out_ref[b * 192:(b + 1) * 192, :] = both.astype(BF)


def gate(normed, flip, wa_ref, wb_ref, cot_ref, gated_ref, keep_ref, send_ref):
    first = jnp.dot(normed, wa_ref[...], preferred_element_type=F32)
    second = jax.nn.sigmoid(jnp.dot(normed, wb_ref[...], preferred_element_type=F32))
    gated = first * second
    gated_ref[...] = gated.astype(BF)
    upstream = cot_ref[...].astype(F32)
    da = (upstream * second).astype(BF)
    db = (upstream * gated * (1.0 - second)).astype(BF)
    for h, slope in enumerate((da, db)):
        grad = jnp.dot(flip, slope, preferred_element_type=F32).astype(BF)
        for d in range(8):
            keep_ref[d, h] = grad[d * 64:d * 64 + 64]
            send_ref[d, h] = grad[d * 64 + 512:d * 64 + 576]


def first_kernel(pos_ref, got_ref, wa_ref, wb_ref, cot_ref, gated_ref, keep_ref, send_ref, normed_ref, flip_ref):
    @pl.when(pl.program_id(0) == 0)
    def _():
        low, high = spread(0), spread(1)
        for b in range(6):
            part = got_ref[b * 192:(b + 1) * 192, :]
            normed_ref[b * 96:(b + 1) * 96, :512] = jnp.dot(low, part, preferred_element_type=F32).astype(BF)
            normed_ref[b * 96:(b + 1) * 96, 512:] = jnp.dot(high, part, preferred_element_type=F32).astype(BF)
        for f in range(0, 16, 2):
            turned = normed_ref[:, f * 64:f * 64 + 128].T
            flip_ref[pos_ref[f]] = turned[:64]
            flip_ref[pos_ref[f + 1]] = turned[64:]

    flip = flip_ref[...].reshape(1024, 576)
    gate(normed_ref[...], flip, wa_ref, wb_ref, cot_ref, gated_ref, keep_ref, send_ref)


def second_kernel(pos_ref, normed_ref, flip_ref, wa_ref, wb_ref, cot_ref, _, gated_ref, keep_ref, send_ref):
    flip = flip_ref[...].reshape(1024, 576)
    gate(normed_ref[...], flip, wa_ref, wb_ref, cot_ref, gated_ref, keep_ref, send_ref)


COLS = 256
STEPS = 512 // COLS


def half_call(pos, lead, w, cot, gated=None):
    second = gated is not None
    fixed = lambda shape: pl.BlockSpec(shape, lambda j, p: (0,) * len(shape))
    wide = pl.BlockSpec((576, COLS), lambda j, p: (0, p[16] * STEPS + j))
    grad = pl.BlockSpec((8, 2, 64, COLS), lambda j, p: (0, 0, 0, j))
    in_specs = [fixed(a.shape) for a in lead]
    in_specs += [pl.BlockSpec((1024, COLS), lambda j, p: (0, j)), pl.BlockSpec((1024, COLS), lambda j, p: (0, j + STEPS)), wide]
    out_specs = [wide] + [grad] * 2
    out_shape = [jax.ShapeDtypeStruct((576, 1024), BF)] + [jax.ShapeDtypeStruct((8, 2, 64, 512), BF)] * 2
    args = [pos, *lead, w, w, cot]
    alias = {}
    if second:
        in_specs.append(pl.BlockSpec(memory_space=pl.ANY))
        alias = {len(args): 0}
        args.append(gated)
    else:
        out_specs += [fixed((576, 1024)), fixed((16, 64, 576))]
        out_shape += [jax.ShapeDtypeStruct((576, 1024), BF), jax.ShapeDtypeStruct((16, 64, 576), BF)]
    gs = pltpu.PrefetchScalarGridSpec(num_scalar_prefetch=1, grid=(STEPS,), in_specs=in_specs, out_specs=out_specs)
    return pl.pallas_call(
        second_kernel if second else first_kernel,
        grid_spec=gs,
        out_shape=out_shape,
        input_output_aliases=alias,
        compiler_params=pltpu.CompilerParams(vmem_limit_bytes=40 << 20),
        name="second" if second else "first",
    )(*args)


def total(*parts):
    acc = parts[0].astype(F32)
    for part in parts[1:]:
        acc = acc + part.astype(F32)
    return acc.astype(BF)


def after(value, other):
    return lax.optimization_barrier((value, other))[0]


def body(frames, route, valid, w_pw, cotangent):
    y, c = lax.axis_index("y"), lax.axis_index("c")
    swap = [(0, 1), (1, 0)]
    shift = lambda d: [(i, (i + d) % 8) for i in range(8)]

    mate = lax.ppermute(w_pw, "c", swap)
    rows = jnp.where(c == 0, jnp.concatenate([w_pw, mate]), jnp.concatenate([mate, w_pw]))
    quarter = [rows[:, q * 512:(q + 1) * 512] for q in range(4)]
    mine = jnp.concatenate([jnp.where(c == 0, quarter[0], quarter[1]), jnp.where(c == 0, quarter[2], quarter[3])], axis=1)

    out = pl.pallas_call(
        pick_kernel,
        out_shape=jax.ShapeDtypeStruct((1152, 512), BF),
        compiler_params=pltpu.CompilerParams(vmem_limit_bytes=30 << 20),
        name="pick",
    )(route[0], valid[0], frames[0, 0])
    got = lax.all_to_all(out.reshape(48, 24, 512), ("z", "x"), 0, 0, tiled=True).reshape(1152, 512)

    w_own = jnp.zeros((8, 128, 1024), BF)
    place = lambda buf, piece, d, at=0: lax.dynamic_update_slice(buf, piece[None], ((y + d) & 7, at, 0))
    w_own = place(w_own, mine, 0)
    up = down = mine
    for step in range(1, 4):
        up = lax.ppermute(up, "y", shift(1))
        down = lax.ppermute(down, "y", shift(-1))
        w_own = place(place(w_own, up, -step), down, step)
    up = lax.ppermute(up[:64], "y", shift(1))
    down = lax.ppermute(down[64:], "y", shift(-1))
    w_own = place(place(w_own, up, 4), down, 4, 64).reshape(1024, 1024)
    w_mate = lax.ppermute(w_own, "c", swap)

    f = jnp.arange(16, dtype=jnp.int32)
    pos = ((f & 1) ^ c) * 8 + (((f >> 1) - y) & 7)
    pos_own = jnp.concatenate([pos, c[None]]).astype(jnp.int32)
    pos_mate = jnp.concatenate([pos, 1 - c[None]]).astype(jnp.int32)
    cot = cotangent[0, 0]
    gated, own, send_own, normed, flip = half_call(pos_own, (got,), w_own, cot)
    got_other = lax.ppermute(send_own, "c", swap)
    gated, other, send_other = half_call(pos_mate, (normed, flip), w_mate, cot, gated)
    got_own = lax.ppermute(send_other, "c", swap)
    near, far = (lambda d: (own[d], got_own[d])), (lambda d: (other[d], got_other[d]))
    up = lax.ppermute(total(*far(4)), "y", shift(1))
    down = lax.ppermute(total(*near(4)), "y", shift(-1))
    for step in range(2, 5):
        d = 5 - step
        if step == 2:
            up = jnp.concatenate([total(*near(d)), total(*far(d), up)])
            down = after(down, up)
            down = jnp.concatenate([total(*near(8 - d), down), total(*far(8 - d))])
        else:
            up = after(up, down_sent)
            up = jnp.concatenate([total(*near(d), up[:2]), total(*far(d), up[2:])])
            down = after(down, up)
            down = jnp.concatenate([total(*near(8 - d), down[:2]), total(*far(8 - d), down[2:])])
        down_sent = down
        up = lax.ppermute(up, "y", shift(1))
        down = lax.ppermute(down, "y", shift(-1))
    oa, ob = total(*near(0), up[:2], down[:2])
    ma, mb = total(*far(0), up[2:], down[2:])
    grad = jnp.where(c == 0, jnp.concatenate([oa, ma, ob, mb], axis=1), jnp.concatenate([ma, oa, mb, ob], axis=1))
    return gated[None, None], grad[None]


def solution(mesh):
    fine = Mesh(mesh.devices.reshape(12, 4, 8, 2), ("z", "x", "y", "c"))
    dp, fsdp = ("z", "x"), ("y", "c")
    in_specs = (P(dp, fsdp), P(dp, fsdp), P(dp, fsdp), P(fsdp), P(dp, fsdp))
    return jax.shard_map(body, mesh=fine, in_specs=in_specs, out_specs=(P(dp, fsdp), P(dp, fsdp)), check_vma=False)
```

```python
import jax
import jax.numpy as jnp
from jax import lax
from jax.experimental import pallas as pl
from jax.experimental.pallas import tpu as pltpu
from jax.sharding import Mesh, PartitionSpec as P


BF, F32 = jnp.bfloat16, jnp.float32
COLS = 256
STEPS = 1024 // COLS


def spread(half, transposed=False):
    shape = (192, 96) if transposed else (96, 192)
    narrow = lax.broadcasted_iota(jnp.int32, shape, 1 if transposed else 0)
    wide = lax.broadcasted_iota(jnp.int32, shape, 0 if transposed else 1)
    hit = wide == narrow + (narrow // 12 + half) * 12
    return jnp.where(hit, 1.0, 0.0).astype(BF)


def pick_kernel(route_hbm, valid_hbm, frames_hbm, out_ref, route_ref, valid_ref, frames_ref, sems):
    copies = [
        pltpu.make_async_copy(src, dst, sems.at[i])
        for i, (src, dst) in enumerate(((route_hbm, route_ref), (valid_hbm, valid_ref), (frames_hbm, frames_ref)))
    ]
    for copy in copies:
        copy.start()
    rows = frames_ref.shape[0]
    lane = lax.broadcasted_iota(jnp.int32, (rows, rows), 1)
    sub = lax.broadcasted_iota(jnp.int32, (rows, rows), 0)
    copies[0].wait()
    order = jnp.sum(jnp.where(lane == sub, route_ref[...].astype(F32), 0.0), axis=1, keepdims=True)
    copies[1].wait()
    hit = (lane == order.astype(jnp.int32)) & (valid_ref[...] > 0)
    chosen = jnp.where(hit, 1.0, 0.0).astype(BF)
    copies[2].wait()
    values = jnp.dot(chosen, frames_ref[...], preferred_element_type=F32)
    mean = jnp.mean(values, axis=-1, keepdims=True)
    centred = values - mean
    variance = jnp.mean(centred * centred, axis=-1, keepdims=True)
    normed = (centred * lax.rsqrt(variance + 1e-05)).astype(BF)
    even = jnp.concatenate([normed[:, j * 128:j * 128 + 64] for j in range(8)], axis=1)
    odd = jnp.concatenate([normed[:, j * 128 + 64:j * 128 + 128] for j in range(8)], axis=1)
    low, high = spread(0, True), spread(1, True)
    for b in range(rows // 96):
        both = jnp.dot(low, even[b * 96:(b + 1) * 96], preferred_element_type=F32)
        both += jnp.dot(high, odd[b * 96:(b + 1) * 96], preferred_element_type=F32)
        out_ref[b * 192:(b + 1) * 192, :] = both.astype(BF)


def main_kernel(
    pos_ref, got_ref, own_a, own_b, mate_a, mate_b, cot_ref,
    gated_ref, keep_ref, far_ref, send_ref, normed_ref, flip_ref,
):
    @pl.when(pl.program_id(0) == 0)
    def _():
        for h in range(2):
            chosen = spread(h)
            for b in range(6):
                part = got_ref[b * 192:(b + 1) * 192, :]
                normed_ref[h, b * 96:(b + 1) * 96, :] = jnp.dot(chosen, part, preferred_element_type=F32).astype(BF)
            for j in range(4):
                turned = normed_ref[h, :, j * 128:j * 128 + 128].T
                flip_ref[pos_ref[4 * j + h]] = turned[:64]
                flip_ref[pos_ref[4 * j + 2 + h]] = turned[64:]

    core = pos_ref[16]
    own, mate = normed_ref[core], normed_ref[1 - core]
    dot = lambda u, v: jnp.dot(u, v, preferred_element_type=F32)
    first = dot(own, own_a[...]) + dot(mate, mate_a[...])
    second = jax.nn.sigmoid(dot(own, own_b[...]) + dot(mate, mate_b[...]))
    gated = first * second
    gated_ref[...] = gated.astype(BF)
    upstream = cot_ref[...].astype(F32)
    flip = flip_ref[...].reshape(1024, 576)
    da = (upstream * second).astype(BF)
    db = (upstream * gated * (1.0 - second)).astype(BF)
    for h, slope in enumerate((da, db)):
        grad = dot(flip, slope).astype(BF)
        for d in range(8):
            keep_ref[d, h] = grad[d * 64:d * 64 + 64]
            block = grad[d * 64 + 512:d * 64 + 576]
            if d == 4:
                far_ref[h] = block
            else:
                send_ref[d - (d > 4), h] = block


def main_call(pos, got, own, mate, cot):
    half = lambda shift: pl.BlockSpec((512, COLS), lambda j, p: (0, j + shift))
    wide = pl.BlockSpec((576, COLS), lambda j, p: (0, j))
    gs = pltpu.PrefetchScalarGridSpec(
        num_scalar_prefetch=1,
        grid=(STEPS,),
        in_specs=[pl.BlockSpec((1152, 512), lambda j, p: (0, 0)), half(0), half(STEPS), half(0), half(STEPS), wide],
        out_specs=[
            wide,
            pl.BlockSpec((8, 2, 64, COLS), lambda j, p: (0, 0, 0, j)),
            pl.BlockSpec((2, 64, COLS), lambda j, p: (0, 0, j)),
            pl.BlockSpec((7, 2, 64, COLS), lambda j, p: (0, 0, 0, j)),
        ],
        scratch_shapes=[pltpu.VMEM((2, 576, 512), BF), pltpu.VMEM((16, 64, 576), BF)],
    )
    return pl.pallas_call(
        main_kernel,
        grid_spec=gs,
        out_shape=[
            jax.ShapeDtypeStruct((576, 1024), BF),
            jax.ShapeDtypeStruct((8, 2, 64, 1024), BF),
            jax.ShapeDtypeStruct((2, 64, 1024), BF),
            jax.ShapeDtypeStruct((7, 2, 64, 1024), BF),
        ],
        compiler_params=pltpu.CompilerParams(vmem_limit_bytes=40 << 20),
        name="main",
    )(pos, got, own, own, mate, mate, cot)


def total(*parts):
    acc = parts[0].astype(F32)
    for part in parts[1:]:
        acc = acc + part.astype(F32)
    return acc.astype(BF)


def stay(value):
    return pltpu.with_memory_space_constraint(value, pltpu.HBM)


def after(value, other):
    return lax.optimization_barrier((value, other))[0]


def body(frames, route, valid, w_pw, cotangent):
    y, c = lax.axis_index("y"), lax.axis_index("c")
    swap = [(0, 1), (1, 0)]
    ring = lambda d: [(i, (i + d) % 8) for i in range(8)]

    def pass_on(up, down):
        up = lax.ppermute(up, "y", ring(1))
        down = lax.ppermute(down, "y", ring(-1))
        return up, down

    up, down = pass_on(w_pw, w_pw)
    anywhere = pl.BlockSpec(memory_space=pltpu.HBM)
    out = pl.pallas_call(
        pick_kernel,
        in_specs=[anywhere] * 3,
        out_shape=jax.ShapeDtypeStruct((1152, 512), BF),
        scratch_shapes=[
            pltpu.VMEM((1, 576), jnp.int32),
            pltpu.VMEM((1, 576), jnp.int32),
            pltpu.VMEM((576, 1024), BF),
            pltpu.SemaphoreType.DMA((3,)),
        ],
        compiler_params=pltpu.CompilerParams(vmem_limit_bytes=30 << 20),
        name="pick",
    )(stay(route[0]), stay(valid[0]), stay(frames[0, 0]))
    got = lax.all_to_all(out.reshape(48, 24, 512), ("z", "x"), 0, 0, tiled=True).reshape(1152, 512)

    own = jnp.zeros((8, 64, 2048), BF)
    place = lambda buf, piece, d, at=0: lax.dynamic_update_slice(buf, piece[None], ((y + d) & 7, at, 0))
    own = place(own, w_pw, 0)
    for step in range(2, 5):
        own = place(place(own, up, 1 - step), down, step - 1)
        up, down = pass_on(up if step < 4 else up[:32], down if step < 4 else down[32:])
    own = place(place(own, up, 4), down, 4, 32).reshape(512, 2048)
    mate = lax.ppermute(own, "c", swap)

    f = jnp.arange(16, dtype=jnp.int32)
    pos = ((f & 1) ^ c) * 8 + (((f >> 1) - y) & 7)
    pos = jnp.concatenate([pos, c[None]]).astype(jnp.int32)
    gated, keep, far, rest = main_call(pos, got, own, mate, stay(cotangent[0, 0]))

    far = lax.ppermute(far, "c", swap)
    rest = lax.ppermute(rest, "c", swap)
    piece = lambda d: (keep[d], rest[d - (d > 4)])
    mid = total(keep[4], far)
    up, down = pass_on(mid[0], mid[1])
    k, g = piece(3)
    up = jnp.stack([total(k[0], g[0], up), total(k[1], g[1])])
    k, g = piece(5)
    down = after(down, up)
    down = jnp.stack([total(k[0], g[0]), total(k[1], g[1], down)])
    for d in (2, 1, 0):
        sent = down
        up, down = pass_on(up, down)
        if d:
            up = total(*piece(d), after(up, sent))
            down = total(*piece(8 - d), after(down, up))
    grad = total(*piece(0), up, down)
    grad = jnp.concatenate([grad[0], grad[1]], axis=1)
    return gated[None, None], grad[None]


def solution(mesh):
    fine = Mesh(mesh.devices.reshape(12, 4, 8, 2), ("z", "x", "y", "c"))
    dp, fsdp = ("z", "x"), ("y", "c")
    in_specs = (P(dp, fsdp), P(dp, fsdp), P(dp, fsdp), P(fsdp), P(dp, fsdp))
    return jax.shard_map(body, mesh=fine, in_specs=in_specs, out_specs=(P(dp, fsdp), P(dp, fsdp)), check_vma=False)
```

```python
import jax
import jax.numpy as jnp
from jax import lax
from jax.experimental import pallas as pl
from jax.experimental.pallas import tpu as pltpu
from jax.sharding import Mesh, PartitionSpec as P


BF, F32 = jnp.bfloat16, jnp.float32
COLS = 256
STEPS = 1024 // COLS


def spread(half, transposed=False):
    shape = (192, 96) if transposed else (96, 192)
    narrow = lax.broadcasted_iota(jnp.int32, shape, 1 if transposed else 0)
    wide = lax.broadcasted_iota(jnp.int32, shape, 0 if transposed else 1)
    hit = wide == narrow + (narrow // 12 + half) * 12
    return jnp.where(hit, 1.0, 0.0).astype(BF)


def pick_kernel(route_hbm, valid_hbm, frames_hbm, out_ref, route_ref, valid_ref, frames_ref, sems):
    copies = [
        pltpu.make_async_copy(src, dst, sems.at[i])
        for i, (src, dst) in enumerate(((route_hbm, route_ref), (valid_hbm, valid_ref), (frames_hbm, frames_ref)))
    ]
    for copy in copies:
        copy.start()
    rows = frames_ref.shape[0]
    lane = lax.broadcasted_iota(jnp.int32, (rows, rows), 1)
    sub = lax.broadcasted_iota(jnp.int32, (rows, rows), 0)
    copies[0].wait()
    order = jnp.sum(jnp.where(lane == sub, route_ref[...].astype(F32), 0.0), axis=1, keepdims=True)
    copies[1].wait()
    hit = (lane == order.astype(jnp.int32)) & (valid_ref[...] > 0)
    chosen = jnp.where(hit, 1.0, 0.0).astype(BF)
    copies[2].wait()
    values = jnp.dot(chosen, frames_ref[...], preferred_element_type=F32)
    mean = jnp.mean(values, axis=-1, keepdims=True)
    centred = values - mean
    variance = jnp.mean(centred * centred, axis=-1, keepdims=True)
    normed = (centred * lax.rsqrt(variance + 1e-05)).astype(BF)
    even = jnp.concatenate([normed[:, j * 128:j * 128 + 64] for j in range(8)], axis=1)
    odd = jnp.concatenate([normed[:, j * 128 + 64:j * 128 + 128] for j in range(8)], axis=1)
    low, high = spread(0, True), spread(1, True)
    for b in range(rows // 96):
        both = jnp.dot(low, even[b * 96:(b + 1) * 96], preferred_element_type=F32)
        both += jnp.dot(high, odd[b * 96:(b + 1) * 96], preferred_element_type=F32)
        out_ref[b * 192:(b + 1) * 192, :] = both.astype(BF)


def main_kernel(
    pos_ref, got_ref, own_a, own_b, mate_a, mate_b, cot_ref,
    gated_ref, keep_ref, far_ref, send_ref, normed_ref, flip_ref,
):
    @pl.when(pl.program_id(0) == 0)
    def _():
        for h in range(2):
            chosen = spread(h)
            for b in range(6):
                part = got_ref[b * 192:(b + 1) * 192, :]
                normed_ref[h, b * 96:(b + 1) * 96, :] = jnp.dot(chosen, part, preferred_element_type=F32).astype(BF)
            for j in range(4):
                turned = normed_ref[h, :, j * 128:j * 128 + 128].T
                flip_ref[pos_ref[4 * j + h]] = turned[:64]
                flip_ref[pos_ref[4 * j + 2 + h]] = turned[64:]

    core = pos_ref[16]
    own, mate = normed_ref[core], normed_ref[1 - core]
    dot = lambda u, v: jnp.dot(u, v, preferred_element_type=F32)
    first = dot(own, own_a[...]) + dot(mate, mate_a[...])
    second = jax.nn.sigmoid(dot(own, own_b[...]) + dot(mate, mate_b[...]))
    gated = first * second
    gated_ref[...] = gated.astype(BF)
    upstream = cot_ref[...].astype(F32)
    flip = flip_ref[...].reshape(1024, 576)
    da = (upstream * second).astype(BF)
    db = (upstream * gated * (1.0 - second)).astype(BF)
    for h, slope in enumerate((da, db)):
        grad = dot(flip, slope).astype(BF)
        for d in range(8):
            keep_ref[d, h] = grad[d * 64:d * 64 + 64]
            block = grad[d * 64 + 512:d * 64 + 576]
            if d == 4:
                far_ref[h] = block
            else:
                send_ref[d - (d > 4), h] = block


def main_call(pos, got, own, mate, cot):
    half = lambda shift: pl.BlockSpec((512, COLS), lambda j, p: (0, j + shift))
    wide = pl.BlockSpec((576, COLS), lambda j, p: (0, j))
    gs = pltpu.PrefetchScalarGridSpec(
        num_scalar_prefetch=1,
        grid=(STEPS,),
        in_specs=[pl.BlockSpec((1152, 512), lambda j, p: (0, 0)), half(0), half(STEPS), half(0), half(STEPS), wide],
        out_specs=[
            wide,
            pl.BlockSpec((8, 2, 64, COLS), lambda j, p: (0, 0, 0, j)),
            pl.BlockSpec((2, 64, COLS), lambda j, p: (0, 0, j)),
            pl.BlockSpec((7, 2, 64, COLS), lambda j, p: (0, 0, 0, j)),
        ],
        scratch_shapes=[pltpu.VMEM((2, 576, 512), BF), pltpu.VMEM((16, 64, 576), BF)],
    )
    return pl.pallas_call(
        main_kernel,
        grid_spec=gs,
        out_shape=[
            jax.ShapeDtypeStruct((576, 1024), BF),
            jax.ShapeDtypeStruct((8, 2, 64, 1024), BF),
            jax.ShapeDtypeStruct((2, 64, 1024), BF),
            jax.ShapeDtypeStruct((7, 2, 64, 1024), BF),
        ],
        compiler_params=pltpu.CompilerParams(vmem_limit_bytes=40 << 20),
        name="main",
    )(pos, got, own, own, mate, mate, cot)


def total(*parts):
    acc = parts[0].astype(F32)
    for part in parts[1:]:
        acc = acc + part.astype(F32)
    return acc.astype(BF)


def stay(value):
    return pltpu.with_memory_space_constraint(value, pltpu.HBM)


def after(value, other):
    return lax.optimization_barrier((value, other))[0]


def body(frames, route, valid, w_pw, cotangent):
    y, c = lax.axis_index("y"), lax.axis_index("c")
    swap = [(0, 1), (1, 0)]
    ring = lambda d: [(i, (i + d) % 8) for i in range(8)]

    def pass_on(up, down):
        up = lax.ppermute(up, "y", ring(1))
        down = lax.ppermute(down, "y", ring(-1))
        return up, down

    across = lax.ppermute(w_pw, "y", ring(4))
    anywhere = pl.BlockSpec(memory_space=pltpu.HBM)
    out = pl.pallas_call(
        pick_kernel,
        in_specs=[anywhere] * 3,
        out_shape=jax.ShapeDtypeStruct((1152, 512), BF),
        scratch_shapes=[
            pltpu.VMEM((1, 576), jnp.int32),
            pltpu.VMEM((1, 576), jnp.int32),
            pltpu.VMEM((576, 1024), BF),
            pltpu.SemaphoreType.DMA((3,)),
        ],
        compiler_params=pltpu.CompilerParams(vmem_limit_bytes=30 << 20),
        name="pick",
    )(stay(route[0]), stay(valid[0]), stay(frames[0, 0]))
    got = lax.all_to_all(out.reshape(48, 24, 512), ("z", "x"), 0, 0, tiled=True).reshape(1152, 512)

    own = jnp.zeros((8, 64, 2048), BF)
    place = lambda buf, piece, d, at=0: lax.dynamic_update_slice(buf, piece[None], ((y + d) & 7, at, 0))
    own = place(own, w_pw, 0)
    own = place(own, across, 4)
    both = jnp.stack([w_pw, across])
    up, down = pass_on(both, both)
    own = place(place(place(place(own, up[0], -1), up[1], 3), down[0], 1), down[1], -3)
    up, down = pass_on(up[0], down[0])
    own = place(place(own, up, -2), down, 2).reshape(512, 2048)
    mate = lax.ppermute(own, "c", swap)

    f = jnp.arange(16, dtype=jnp.int32)
    pos = ((f & 1) ^ c) * 8 + (((f >> 1) - y) & 7)
    pos = jnp.concatenate([pos, c[None]]).astype(jnp.int32)
    gated, keep, far, rest = main_call(pos, got, own, mate, stay(cotangent[0, 0]))

    far = lax.ppermute(far, "c", swap)
    rest = lax.ppermute(rest, "c", swap)
    piece = lambda d: (keep[d], rest[d - (d > 4)])
    mid = total(keep[4], far)
    up, down = pass_on(mid[0], mid[1])
    k, g = piece(3)
    up = jnp.stack([total(k[0], g[0], up), total(k[1], g[1])])
    k, g = piece(5)
    down = after(down, up)
    down = jnp.stack([total(k[0], g[0]), total(k[1], g[1], down)])
    for d in (2, 1, 0):
        sent = down
        up, down = pass_on(up, down)
        if d:
            up = total(*piece(d), after(up, sent))
            down = total(*piece(8 - d), after(down, up))
    grad = total(*piece(0), up, down)
    grad = jnp.concatenate([grad[0], grad[1]], axis=1)
    return gated[None, None], grad[None]


def solution(mesh):
    fine = Mesh(mesh.devices.reshape(12, 4, 8, 2), ("z", "x", "y", "c"))
    dp, fsdp = ("z", "x"), ("y", "c")
    in_specs = (P(dp, fsdp), P(dp, fsdp), P(dp, fsdp), P(fsdp), P(dp, fsdp))
    return jax.shard_map(body, mesh=fine, in_specs=in_specs, out_specs=(P(dp, fsdp), P(dp, fsdp)), check_vma=False)
```

```python
import jax
import jax.numpy as jnp
from jax import lax
from jax.experimental import pallas as pl
from jax.experimental.pallas import tpu as pltpu
from jax.sharding import Mesh, PartitionSpec as P


BF, F32 = jnp.bfloat16, jnp.float32
COLS = 256
STEPS = 1024 // COLS


def spread(half, transposed=False):
    shape = (192, 96) if transposed else (96, 192)
    narrow = lax.broadcasted_iota(jnp.int32, shape, 1 if transposed else 0)
    wide = lax.broadcasted_iota(jnp.int32, shape, 0 if transposed else 1)
    hit = wide == narrow + (narrow // 12 + half) * 12
    return jnp.where(hit, 1.0, 0.0).astype(BF)


def pick_kernel(route_hbm, valid_hbm, frames_hbm, out_ref, route_ref, valid_ref, frames_ref, sems):
    copies = [
        pltpu.make_async_copy(src, dst, sems.at[i])
        for i, (src, dst) in enumerate(((route_hbm, route_ref), (valid_hbm, valid_ref), (frames_hbm, frames_ref)))
    ]
    for copy in copies:
        copy.start()
    rows = frames_ref.shape[0]
    lane = lax.broadcasted_iota(jnp.int32, (rows, rows), 1)
    sub = lax.broadcasted_iota(jnp.int32, (rows, rows), 0)
    copies[0].wait()
    order = jnp.sum(jnp.where(lane == sub, route_ref[...].astype(F32), 0.0), axis=1, keepdims=True)
    copies[1].wait()
    hit = (lane == order.astype(jnp.int32)) & (valid_ref[...] > 0)
    chosen = jnp.where(hit, 1.0, 0.0).astype(BF)
    copies[2].wait()
    values = jnp.dot(chosen, frames_ref[...], preferred_element_type=F32)
    mean = jnp.mean(values, axis=-1, keepdims=True)
    centred = values - mean
    variance = jnp.mean(centred * centred, axis=-1, keepdims=True)
    normed = (centred * lax.rsqrt(variance + 1e-05)).astype(BF)
    even = jnp.concatenate([normed[:, j * 128:j * 128 + 64] for j in range(8)], axis=1)
    odd = jnp.concatenate([normed[:, j * 128 + 64:j * 128 + 128] for j in range(8)], axis=1)
    low, high = spread(0, True), spread(1, True)
    for b in range(rows // 96):
        both = jnp.dot(low, even[b * 96:(b + 1) * 96], preferred_element_type=F32)
        both += jnp.dot(high, odd[b * 96:(b + 1) * 96], preferred_element_type=F32)
        out_ref[b * 192:(b + 1) * 192, :] = both.astype(BF)


def main_kernel(
    pos_ref, got_ref, own_a, own_b, mate_a, mate_b, cot_ref,
    gated_ref, keep_ref, far_ref, send_ref, normed_ref, flip_ref,
):
    @pl.when(pl.program_id(0) == 0)
    def _():
        for h in range(2):
            chosen = spread(h)
            for b in range(6):
                part = got_ref[b * 192:(b + 1) * 192, :]
                normed_ref[h, b * 96:(b + 1) * 96, :] = jnp.dot(chosen, part, preferred_element_type=F32).astype(BF)
            for j in range(4):
                turned = normed_ref[h, :, j * 128:j * 128 + 128].T
                flip_ref[pos_ref[4 * j + h]] = turned[:64]
                flip_ref[pos_ref[4 * j + 2 + h]] = turned[64:]

    core = pos_ref[16]
    own, mate = normed_ref[core], normed_ref[1 - core]
    dot = lambda u, v: jnp.dot(u, v, preferred_element_type=F32)
    first = dot(own, own_a[...]) + dot(mate, mate_a[...])
    second = jax.nn.sigmoid(dot(own, own_b[...]) + dot(mate, mate_b[...]))
    gated = first * second
    gated_ref[...] = gated.astype(BF)
    upstream = cot_ref[...].astype(F32)
    flip = flip_ref[...].reshape(1024, 576)
    da = (upstream * second).astype(BF)
    db = (upstream * gated * (1.0 - second)).astype(BF)
    for h, slope in enumerate((da, db)):
        grad = dot(flip, slope).astype(BF).reshape(16, 64, COLS)
        keep_ref[h] = grad[:8]
        far_ref[h] = grad[8]
        send_ref[h] = grad[9:]


def main_call(pos, got, own, mate, cot):
    half = lambda shift: pl.BlockSpec((512, COLS), lambda j, p: (0, j + shift))
    wide = pl.BlockSpec((576, COLS), lambda j, p: (0, j))
    gs = pltpu.PrefetchScalarGridSpec(
        num_scalar_prefetch=1,
        grid=(STEPS,),
        in_specs=[pl.BlockSpec((1152, 512), lambda j, p: (0, 0)), half(0), half(STEPS), half(0), half(STEPS), wide],
        out_specs=[
            wide,
            pl.BlockSpec((2, 8, 64, COLS), lambda j, p: (0, 0, 0, j)),
            pl.BlockSpec((2, 64, COLS), lambda j, p: (0, 0, j)),
            pl.BlockSpec((2, 7, 64, COLS), lambda j, p: (0, 0, 0, j)),
        ],
        scratch_shapes=[pltpu.VMEM((2, 576, 512), BF), pltpu.VMEM((16, 64, 576), BF)],
    )
    return pl.pallas_call(
        main_kernel,
        grid_spec=gs,
        out_shape=[
            jax.ShapeDtypeStruct((576, 1024), BF),
            jax.ShapeDtypeStruct((2, 8, 64, 1024), BF),
            jax.ShapeDtypeStruct((2, 64, 1024), BF),
            jax.ShapeDtypeStruct((2, 7, 64, 1024), BF),
        ],
        compiler_params=pltpu.CompilerParams(vmem_limit_bytes=40 << 20),
        name="main",
    )(pos, got, own, own, mate, mate, cot)


def total(*parts):
    acc = parts[0].astype(F32)
    for part in parts[1:]:
        acc = acc + part.astype(F32)
    return acc.astype(BF)


def stay(value):
    return pltpu.with_memory_space_constraint(value, pltpu.HBM)


def after(value, other):
    return lax.optimization_barrier((value, other))[0]


def body(frames, route, valid, w_pw, cotangent):
    y, c = lax.axis_index("y"), lax.axis_index("c")
    swap = [(0, 1), (1, 0)]
    ring = lambda d: [(i, (i + d) % 8) for i in range(8)]

    def pass_on(up, down):
        up = lax.ppermute(up, "y", ring(1))
        down = lax.ppermute(down, "y", ring(-1))
        return up, down

    across = lax.ppermute(w_pw, "y", ring(4))
    anywhere = pl.BlockSpec(memory_space=pltpu.HBM)
    out = pl.pallas_call(
        pick_kernel,
        in_specs=[anywhere] * 3,
        out_shape=jax.ShapeDtypeStruct((1152, 512), BF),
        scratch_shapes=[
            pltpu.VMEM((1, 576), jnp.int32),
            pltpu.VMEM((1, 576), jnp.int32),
            pltpu.VMEM((576, 1024), BF),
            pltpu.SemaphoreType.DMA((3,)),
        ],
        compiler_params=pltpu.CompilerParams(vmem_limit_bytes=30 << 20),
        name="pick",
    )(stay(route[0]), stay(valid[0]), stay(frames[0, 0]))
    got = lax.all_to_all(out.reshape(48, 24, 512), ("z", "x"), 0, 0, tiled=True).reshape(1152, 512)

    own = jnp.zeros((8, 64, 2048), BF)
    place = lambda buf, piece, d, at=0: lax.dynamic_update_slice(buf, piece[None], ((y + d) & 7, at, 0))
    own = place(own, w_pw, 0)
    own = place(own, across, 4)
    both = jnp.stack([w_pw, across])
    up, down = pass_on(both, both)
    own = place(place(place(place(own, up[0], -1), up[1], 3), down[0], 1), down[1], -3)
    up, down = pass_on(up[0], down[0])
    own = place(place(own, up, -2), down, 2).reshape(512, 2048)
    mate = lax.ppermute(own, "c", swap)

    f = jnp.arange(16, dtype=jnp.int32)
    gap = ((f >> 1) - y) & 7
    gap = jnp.where(c == 0, gap, (8 - gap) & 7)
    ends = (gap & 3) == 0
    turn = (f & 1) ^ c
    theirs = jnp.where(ends, turn, (gap > 4).astype(jnp.int32))
    near = jnp.where(gap > 4, 8 - gap, gap)
    pos = jnp.where(ends, jnp.where(gap == 0, 7, 0), 7 - 2 * near + (turn ^ theirs)) + 8 * theirs
    pos = jnp.concatenate([pos, c[None]]).astype(jnp.int32)
    gated, keep, far, rest = main_call(pos, got, own, mate, stay(cotangent[0, 0]))

    far = lax.ppermute(far, "c", swap)
    rest = lax.ppermute(rest, "c", swap)
    ways = [(2 * i, 2 * ((i + 1) % 8)) for i in range(8)] + [(2 * i + 1, 2 * ((i - 1) % 8) + 1) for i in range(8)]
    got = lax.ppermute(total(keep[:, 0], far), ("y", "c"), ways)
    part = lambda h, i, n=1: (keep[h, i:i + n], rest[h, i - 1:i - 1 + n])
    chains = [got[0][None], got[1][None]]
    sent = None
    for step in range(2, 5):
        for h in range(2):
            got = chains[h] if sent is None else after(chains[h], sent)
            at = 2 * step - 3
            if step == 2:
                sent = jnp.concatenate([total(*part(h, at), got), total(*part(h, at + 1))])
            else:
                sent = total(*part(h, at, 2), got)
            chains[h] = lax.ppermute(sent, ("y", "c"), ways)
    grads = []
    for h in range(2):
        grads.append(total(*part(h, 7), chains[h][:1], lax.ppermute(chains[h][1:], "c", swap))[0])
    grad = jnp.concatenate(grads, axis=1)
    return gated[None, None], grad[None]


def solution(mesh):
    fine = Mesh(mesh.devices.reshape(12, 4, 8, 2), ("z", "x", "y", "c"))
    dp, fsdp = ("z", "x"), ("y", "c")
    in_specs = (P(dp, fsdp), P(dp, fsdp), P(dp, fsdp), P(fsdp), P(dp, fsdp))
    return jax.shard_map(body, mesh=fine, in_specs=in_specs, out_specs=(P(dp, fsdp), P(dp, fsdp)), check_vma=False)
```

```python
import jax
import jax.numpy as jnp
from jax import lax
from jax.experimental import pallas as pl
from jax.experimental.pallas import tpu as pltpu
from jax.sharding import Mesh, PartitionSpec as P


BF, F32 = jnp.bfloat16, jnp.float32
COLS = 1024
STEPS = 1024 // COLS


def spread(half, transposed=False):
    shape = (192, 96) if transposed else (96, 192)
    narrow = lax.broadcasted_iota(jnp.int32, shape, 1 if transposed else 0)
    wide = lax.broadcasted_iota(jnp.int32, shape, 0 if transposed else 1)
    hit = wide == narrow + (narrow // 12 + half) * 12
    return jnp.where(hit, 1.0, 0.0).astype(BF)


def pick_kernel(route_hbm, valid_hbm, frames_hbm, out_ref, route_ref, valid_ref, frames_ref, sems):
    copies = [
        pltpu.make_async_copy(src, dst, sems.at[i])
        for i, (src, dst) in enumerate(((route_hbm, route_ref), (valid_hbm, valid_ref), (frames_hbm, frames_ref)))
    ]
    for copy in copies:
        copy.start()
    rows = frames_ref.shape[0]
    lane = lax.broadcasted_iota(jnp.int32, (rows, rows), 1)
    sub = lax.broadcasted_iota(jnp.int32, (rows, rows), 0)
    copies[0].wait()
    order = jnp.sum(jnp.where(lane == sub, route_ref[...].astype(F32), 0.0), axis=1, keepdims=True)
    copies[1].wait()
    hit = (lane == order.astype(jnp.int32)) & (valid_ref[...] > 0)
    chosen = jnp.where(hit, 1.0, 0.0).astype(BF)
    copies[2].wait()
    values = jnp.dot(chosen, frames_ref[...], preferred_element_type=F32)
    mean = jnp.mean(values, axis=-1, keepdims=True)
    centred = values - mean
    variance = jnp.mean(centred * centred, axis=-1, keepdims=True)
    normed = (centred * lax.rsqrt(variance + 1e-05)).astype(BF)
    even = jnp.concatenate([normed[:, j * 128:j * 128 + 64] for j in range(8)], axis=1)
    odd = jnp.concatenate([normed[:, j * 128 + 64:j * 128 + 128] for j in range(8)], axis=1)
    low, high = spread(0, True), spread(1, True)
    for b in range(rows // 96):
        both = jnp.dot(low, even[b * 96:(b + 1) * 96], preferred_element_type=F32)
        both += jnp.dot(high, odd[b * 96:(b + 1) * 96], preferred_element_type=F32)
        out_ref[b * 192:(b + 1) * 192, :] = both.astype(BF)


def main_kernel(
    pos_ref, got_ref, own_a, own_b, mate_a, mate_b, cot_ref,
    gated_ref, keep_ref, far_ref, send_ref, normed_ref, flip_ref,
):
    @pl.when(pl.program_id(0) == 0)
    def _():
        for h in range(2):
            chosen = spread(h)
            for b in range(6):
                part = got_ref[b * 192:(b + 1) * 192, :]
                normed_ref[h, b * 96:(b + 1) * 96, :] = jnp.dot(chosen, part, preferred_element_type=F32).astype(BF)
            for j in range(4):
                turned = normed_ref[h, :, j * 128:j * 128 + 128].T
                flip_ref[pos_ref[4 * j + h]] = turned[:64]
                flip_ref[pos_ref[4 * j + 2 + h]] = turned[64:]

    core = pos_ref[16]
    own, mate = normed_ref[core], normed_ref[1 - core]
    dot = lambda u, v: jnp.dot(u, v, preferred_element_type=F32)
    first = dot(own, own_a[...]) + dot(mate, mate_a[...])
    second = jax.nn.sigmoid(dot(own, own_b[...]) + dot(mate, mate_b[...]))
    gated = first * second
    gated_ref[...] = gated.astype(BF)
    upstream = cot_ref[...].astype(F32)
    flip = flip_ref[...].reshape(1024, 576)
    da = (upstream * second).astype(BF)
    db = (upstream * gated * (1.0 - second)).astype(BF)
    for h, slope in enumerate((da, db)):
        grad = dot(flip, slope).astype(BF)
        for d in range(8):
            keep_ref[d, h] = grad[d * 64:d * 64 + 64]
            block = grad[d * 64 + 512:d * 64 + 576]
            if d == 4:
                far_ref[h] = block
            else:
                send_ref[d - (d > 4), h] = block


def main_call(pos, got, own, mate, cot):
    half = lambda shift: pl.BlockSpec((512, COLS), lambda j, p: (0, j + shift))
    wide = pl.BlockSpec((576, COLS), lambda j, p: (0, j))
    gs = pltpu.PrefetchScalarGridSpec(
        num_scalar_prefetch=1,
        grid=(STEPS,),
        in_specs=[pl.BlockSpec((1152, 512), lambda j, p: (0, 0)), half(0), half(STEPS), half(0), half(STEPS), wide],
        out_specs=[
            wide,
            pl.BlockSpec((8, 2, 64, COLS), lambda j, p: (0, 0, 0, j)),
            pl.BlockSpec((2, 64, COLS), lambda j, p: (0, 0, j)),
            pl.BlockSpec((7, 2, 64, COLS), lambda j, p: (0, 0, 0, j)),
        ],
        scratch_shapes=[pltpu.VMEM((2, 576, 512), BF), pltpu.VMEM((16, 64, 576), BF)],
    )
    return pl.pallas_call(
        main_kernel,
        grid_spec=gs,
        out_shape=[
            jax.ShapeDtypeStruct((576, 1024), BF),
            jax.ShapeDtypeStruct((8, 2, 64, 1024), BF),
            jax.ShapeDtypeStruct((2, 64, 1024), BF),
            jax.ShapeDtypeStruct((7, 2, 64, 1024), BF),
        ],
        compiler_params=pltpu.CompilerParams(vmem_limit_bytes=40 << 20),
        name="main",
    )(pos, got, own, own, mate, mate, cot)


def total(*parts):
    acc = parts[0].astype(F32)
    for part in parts[1:]:
        acc = acc + part.astype(F32)
    return acc.astype(BF)


def stay(value):
    return pltpu.with_memory_space_constraint(value, pltpu.HBM)


def after(value, other):
    return lax.optimization_barrier((value, other))[0]


def body(frames, route, valid, w_pw, cotangent):
    y, c = lax.axis_index("y"), lax.axis_index("c")
    swap = [(0, 1), (1, 0)]
    ring = lambda d: [(i, (i + d) % 8) for i in range(8)]

    def pass_on(up, down):
        up = lax.ppermute(up, "y", ring(1))
        down = lax.ppermute(down, "y", ring(-1))
        return up, down

    across = lax.ppermute(w_pw, "y", ring(4))
    anywhere = pl.BlockSpec(memory_space=pltpu.HBM)
    out = pl.pallas_call(
        pick_kernel,
        in_specs=[anywhere] * 3,
        out_shape=jax.ShapeDtypeStruct((1152, 512), BF),
        scratch_shapes=[
            pltpu.VMEM((1, 576), jnp.int32),
            pltpu.VMEM((1, 576), jnp.int32),
            pltpu.VMEM((576, 1024), BF),
            pltpu.SemaphoreType.DMA((3,)),
        ],
        compiler_params=pltpu.CompilerParams(vmem_limit_bytes=30 << 20),
        name="pick",
    )(stay(route[0]), stay(valid[0]), stay(frames[0, 0]))
    got = lax.all_to_all(out.reshape(48, 24, 512), ("z", "x"), 0, 0, tiled=True).reshape(1152, 512)

    own = jnp.zeros((8, 64, 2048), BF)
    place = lambda buf, piece, d, at=0: lax.dynamic_update_slice(buf, piece[None], ((y + d) & 7, at, 0))
    own = place(own, w_pw, 0)
    own = place(own, across, 4)
    both = jnp.stack([w_pw, across])
    up, down = pass_on(both, both)
    own = place(place(place(place(own, up[0], -1), up[1], 3), down[0], 1), down[1], -3)
    up, down = pass_on(up[0], down[0])
    own = place(place(own, up, -2), down, 2).reshape(512, 2048)
    mate = lax.ppermute(own, "c", swap)

    f = jnp.arange(16, dtype=jnp.int32)
    pos = ((f & 1) ^ c) * 8 + (((f >> 1) - y) & 7)
    pos = jnp.concatenate([pos, c[None]]).astype(jnp.int32)
    gated, keep, far, rest = main_call(pos, got, own, mate, stay(cotangent[0, 0]))

    far = lax.ppermute(far, "c", swap)
    rest = lax.ppermute(rest, "c", swap)
    piece = lambda d: (keep[d], rest[d - (d > 4)])
    mid = total(keep[4], far)
    across = lax.ppermute(mid, "y", ring(4))
    rest = after(rest, mid)
    up, down = total(*piece(3)), total(*piece(5))
    for d in (2, 1, 0):
        sent = down
        up, down = pass_on(up, down)
        if d:
            up = total(*piece(d), after(up, sent))
            down = total(*piece(8 - d), after(down, up))
    grad = total(*piece(0), across, up, down)
    grad = jnp.concatenate([grad[0], grad[1]], axis=1)
    return gated[None, None], grad[None]


def solution(mesh):
    fine = Mesh(mesh.devices.reshape(12, 4, 8, 2), ("z", "x", "y", "c"))
    dp, fsdp = ("z", "x"), ("y", "c")
    in_specs = (P(dp, fsdp), P(dp, fsdp), P(dp, fsdp), P(fsdp), P(dp, fsdp))
    return jax.shard_map(body, mesh=fine, in_specs=in_specs, out_specs=(P(dp, fsdp), P(dp, fsdp)), check_vma=False)
```
